128 devices in a mesh: dp: 8 (over x, core), space: 16 (over z, y).
Axes of the slice: x: 4, y: 4, z: 4, core: 2. Of those that a mesh axis runs over, the one named last changes fastest.
Arguments:
- features: bfloat16 [8, 192, 72, 2048], P('dp', 'space'), may hold values from -0.10205078 to 0.10205078
- grad_out: bfloat16 [8, 192, 72, 256], P('dp', 'space'), may hold values from -6 to 6
- weight: bfloat16 [18432, 256], replicated, may hold values from -0.125 to 0.125
- alive: int32 [8], P('dp'), may hold values from 0 to 1, as said below
Outputs:
- weight_grad: float32 [18432, 256], P(('dp', 'space'))
- grad_features: bfloat16 [8, 192, 72, 2048], P('dp', 'space')
The draws below stay inside these ranges and needn't reach their ends.
Inputs may be any that keep to these rules, and one draw needn't show every extreme that they name: `alive`: at least one member survives and at least one does not.
All inputs are finite; a program needn't handle non-finite values.
Results may differ from the reference program's by a relative error of at most 0.001.
Values may be sent and summed in bfloat16 or wider, within the bound.
A program may use at most 320 MiB of HBM per device.

```python
import jax
import jax.numpy as jnp
from jax import lax

INPUT_CHANNELS = 2048
OUTPUT_CHANNELS = 256
KERNEL_DILATION = 18
MAP_COLUMNS = 72
MEMBERS = 8
MEMBER_ROWS = 192
MEMBER_PIXELS = 13824


def draw_alive(key, part):
    key_flags, key_keep, key_drop = jax.random.split(key, 3)
    flags = (jax.random.randint(key_flags, (MEMBERS,), 0, 4) > 0).astype(jnp.int32)
    keeper = jax.random.randint(key_keep, (), 0, MEMBERS)
    dropped = (keeper + 1 + jax.random.randint(key_drop, (), 0, MEMBERS - 1)) % MEMBERS
    positions = jnp.arange(MEMBERS)
    flags = jnp.where(positions == keeper, 1, flags)
    flags = jnp.where(positions == dropped, 0, flags)
    return flags.astype(jnp.int32)


def levels(key, extent, shards, low, top_value):
    loudness, own = 1.0, jax.random.fold_in(key, 6)
    for position, shards_of in shards:
        heights = jnp.exp(jax.random.uniform(jax.random.fold_in(own, position), (shards_of,), jnp.float32, low / len(shards), top_value / len(shards)))
        loudness = loudness * jnp.repeat(heights, extent[position] // shards_of).reshape([-1 if axis == position else 1 for axis in range(len(extent))])
    return loudness


def scatter_about(stream_key, extent, scale, limit, cuts=(), dtype=jnp.bfloat16):
    factor_of = levels(stream_key, extent, cuts, -0.22, 0.18) if cuts else 1.0
    array = jax.random.normal(stream_key, extent, jnp.float32) * scale * factor_of
    return jnp.minimum(jnp.maximum(array, -limit), limit).astype(dtype)


def setup_inputs(seed: int = 0) -> dict:
    seeds = jax.random.split(jax.random.key(seed), 5)
    features = scatter_about(seeds[0], (MEMBERS, MEMBER_ROWS, MAP_COLUMNS, INPUT_CHANNELS), (2.0 / MEMBER_PIXELS ** 0.5), 0.10205078, ((0, 8), (1, 16)))
    grad_out = scatter_about(seeds[1], (MEMBERS, MEMBER_ROWS, MAP_COLUMNS, OUTPUT_CHANNELS), 1.0, 6.0, ((0, 8), (1, 16)))
    weight = scatter_about(seeds[2], (INPUT_CHANNELS * 9, OUTPUT_CHANNELS), (9 * OUTPUT_CHANNELS) ** -0.5, 0.125)
    alive = draw_alive(jax.random.fold_in(seeds[4], 71), 0)
    return {"features": features, "grad_out": grad_out, "weight": weight, "alive": alive}


def reference(features, grad_out, weight, alive):
    surviving_members = jnp.sum(alive).astype(jnp.float32)
    member_weighting = alive.astype(jnp.float32) / surviving_members
    tap_weights = weight.reshape(INPUT_CHANNELS, 9, OUTPUT_CHANNELS)
    padding_widths = ((KERNEL_DILATION, KERNEL_DILATION), (KERNEL_DILATION, KERNEL_DILATION), (0, 0))

    def member_step(carry, inputs):
        member_image, upstream, scale_now = inputs
        image_padded = jnp.pad(member_image, padding_widths)
        gradient_padded = jnp.pad(upstream, padding_widths)
        flat_grad = upstream.reshape(MEMBER_PIXELS, OUTPUT_CHANNELS)
        columns = []
        input_grad = jnp.zeros((MEMBER_PIXELS, INPUT_CHANNELS), jnp.float32)
        for tap_index in range(9):
            kernel_tap_row = tap_index // 3
            kernel_tap_column = tap_index % 3
            window_slice = image_padded[kernel_tap_row * KERNEL_DILATION:kernel_tap_row * KERNEL_DILATION + MEMBER_ROWS, kernel_tap_column * KERNEL_DILATION:kernel_tap_column * KERNEL_DILATION + MAP_COLUMNS].reshape(MEMBER_PIXELS, INPUT_CHANNELS)
            columns.append(jnp.dot(window_slice.T, flat_grad, preferred_element_type=jnp.float32))
            shifted_rows = gradient_padded[(2 - kernel_tap_row) * KERNEL_DILATION:(2 - kernel_tap_row) * KERNEL_DILATION + MEMBER_ROWS, (2 - kernel_tap_column) * KERNEL_DILATION:(2 - kernel_tap_column) * KERNEL_DILATION + MAP_COLUMNS].reshape(MEMBER_PIXELS, OUTPUT_CHANNELS)
            input_grad = input_grad + jnp.dot(shifted_rows, tap_weights[:, tap_index, :].T, preferred_element_type=jnp.float32)
        kernel_term = jnp.stack(columns, axis=1).reshape(INPUT_CHANNELS * 9, OUTPUT_CHANNELS)
        carry = carry + scale_now * kernel_term
        member_grad = (input_grad * scale_now).astype(jnp.bfloat16).reshape(MEMBER_ROWS, MAP_COLUMNS, INPUT_CHANNELS)
        return carry, member_grad

    start_grad = jnp.zeros((INPUT_CHANNELS * 9, OUTPUT_CHANNELS), jnp.float32)
    weight_grad, grad_features = lax.scan(member_step, start_grad, (features, grad_out, member_weighting))
    return weight_grad, grad_features
```

```python
import jax
import jax.numpy as jnp
from jax import lax
from jax.sharding import PartitionSpec as P

KERNEL_DILATION = 18


def from_behind(value, axis, steps):
    count = lax.axis_size(axis)
    leading, last = (max(0, -steps), min(count, count - steps))
    return lax.ppermute(value, axis, [(source, source + steps) for source in range(leading, last)])


def shifted_rows(tile):
    rows = tile.shape[1]
    lag, extra = divmod(KERNEL_DILATION, rows)
    keep = rows - extra
    above, below = [], []
    if extra:
        above.append(from_behind(tile[:, keep:], "space", lag + 1))
    above.append(from_behind(tile[:, :keep], "space", lag))
    below.append(from_behind(tile[:, extra:], "space", -lag))
    if extra:
        below.append(from_behind(tile[:, :extra], "space", -(lag + 1)))
    return jnp.concatenate(above, axis=1), jnp.concatenate(below, axis=1)


def tap_matrix(grad):
    members, rows, cols, out_channels = grad.shape
    above, below = shifted_rows(grad)
    blocks = []
    for source in (below, grad, above):
        wide = jnp.pad(source, ((0, 0), (0, 0), (KERNEL_DILATION, KERNEL_DILATION), (0, 0)))
        for kx in range(3):
            start = (2 - kx) * KERNEL_DILATION
            blocks.append(wide[:, :, start : start + cols])
    return jnp.concatenate(blocks, axis=-1).reshape(members * rows * cols, 9 * out_channels)


def shards(features, grad_out, weight, alive):
    members, rows, cols, in_channels = features.shape
    out_channels = grad_out.shape[-1]
    survivors = lax.psum(jnp.sum(alive).astype(jnp.float32), "dp")
    scale = (alive.astype(jnp.float32) / survivors)[0]
    taps = tap_matrix(grad_out)
    flat = features.reshape(rows * cols, in_channels)
    term = lax.dot_general(flat, taps, (((0,), (0,)), ((), ())), preferred_element_type=jnp.float32)
    mine = lax.psum_scatter(term * scale, ("dp", "space"), scatter_dimension=0, tiled=True)
    weight_grad = mine.reshape(-1, out_channels)
    kernel = weight.reshape(in_channels, 9 * out_channels)
    back = lax.dot_general(taps, kernel, (((1,), (1,)), ((), ())), preferred_element_type=jnp.float32)
    grad_features = (back * scale).astype(jnp.bfloat16).reshape(features.shape)
    return weight_grad, grad_features


def solution(mesh):
    in_specs = (P("dp", "space", None, None), P("dp", "space", None, None), P(), P("dp"))
    out_specs = (P(("dp", "space"), None), P("dp", "space", None, None))
    return jax.shard_map(shards, mesh=mesh, in_specs=in_specs, out_specs=out_specs, check_vma=False)
```

```python
import functools

import jax
import jax.numpy as jnp
from jax import lax
from jax.experimental import pallas as pl
from jax.experimental.pallas import tpu as pltpu
from jax.sharding import PartitionSpec as P

KERNEL_DILATION = 18
MESH = pl.DeviceIdType.MESH
F32 = jnp.float32
BF16 = jnp.bfloat16

SIDE = 4
KY_ORDER = (1, 0, 2)
WAVES = ((0, 1), (1, 2))
AXIS_ORDERS = ("xyz", "yzx", "zxy")


def body(
    cols,
    feat, grad, weight, alive,
    wg, gf,
    own_g, par_g, fb, sh, wraw, wf32, wgs, wt, acc, rb1, rb2, rb3, flags, gbuf,
    halo_s, halo_r, fwd_s, fwd_r, cen_s, cen_r, fea_s, fea_r, flag_s, flag_r, st_s, st_r, loc, gf_sem,
):
    pixels = grad.shape[0]
    half = pixels // 2
    out_channels = grad.shape[1]
    width = 3 * out_channels
    block = fb.shape[2]
    dp, space = lax.axis_index("dp"), lax.axis_index("space")
    dp_n, space_n = 2 * SIDE, SIDE * SIDE
    x, k = dp // 2, dp % 2
    z, y = space // SIDE, space % SIDE
    me = {"x": x, "y": y, "z": z}

    def dev(d, s):
        return {"dp": d, "space": s}

    def step(axis, delta):
        moved = dict(me)
        moved[axis] = lax.rem(me[axis] + (delta + SIDE), SIDE)
        return dev(2 * moved["x"] + k, SIDE * moved["z"] + moved["y"])

    def along_space(delta):
        return dev(dp, lax.rem(space + (delta + space_n), space_n))

    def along_dp(delta):
        return dev(lax.rem(dp + delta, dp_n), space)

    partner = dev(2 * x + (1 - k), space)

    barrier = pltpu.get_barrier_semaphore()
    peers = [along_dp(d) for d in range(1, dp_n)]
    peers += [along_space(d) for d in (1, -1, 2, -2)]
    peers += [step(a, d) for a in "yz" for d in (1, -1)]
    for p in peers:
        pl.semaphore_signal(barrier, inc=1, device_id=p, device_id_type=MESH)
    pl.semaphore_wait(barrier, len(peers))

    def remote(src, dst, s_sem, r_sem, to):
        return pltpu.make_async_remote_copy(
            src_ref=src, dst_ref=dst, send_sem=s_sem, recv_sem=r_sem, device_id=to, device_id_type=MESH
        )

    first, last = pl.ds(0, half), pl.ds(half, half)
    halos = [
        remote(grad.at[last], own_g.at[1, first], halo_s.at[0], halo_r.at[0], along_space(-1)),
        remote(grad.at[first], own_g.at[1, last], halo_s.at[1], halo_r.at[1], along_space(-2)),
        remote(grad.at[last], own_g.at[2, first], halo_s.at[2], halo_r.at[2], along_space(2)),
        remote(grad.at[first], own_g.at[2, last], halo_s.at[3], halo_r.at[3], along_space(1)),
    ]
    for c in halos:
        c.start()
    centre = remote(grad, par_g.at[0], cen_s, cen_r, partner)
    centre.start()
    flag_copies = [
        remote(alive, flags.at[d - 1], flag_s.at[d - 1], flag_r.at[d - 1], along_dp(d)) for d in range(1, dp_n)
    ]
    for c in flag_copies:
        c.start()

    def feature_block(v, kk):
        return feat.at[:, pl.ds(pl.multiple_of((2 * v + kk) * block, block), block)]

    own_grad = pltpu.make_async_copy(grad, own_g.at[0], loc.at[0])
    own_grad.start()
    features = []
    for v in range(SIDE):
        c = remote(feature_block(v, 1 - k), fb.at[v, pl.ds(pixels, pixels)], fea_s.at[v], fea_r.at[v], partner)
        c.start()
        own = pltpu.make_async_copy(feature_block(v, k), fb.at[v, pl.ds(0, pixels)], loc.at[2 + v])
        own.start()
        features += [c, own]
    weights = pltpu.make_async_copy(weight, wraw, loc.at[1])
    weights.start()

    pair = 2 * cols
    position = lax.broadcasted_iota(jnp.int32, (pair, out_channels), 0)
    column = jnp.where(position >= cols, position - cols, position)
    keep_low = column < cols - KERNEL_DILATION
    keep_high = column >= KERNEL_DILATION

    def build(source, base, ky, factor, start, stop):
        def rows(i, _):
            at = pl.ds(pl.multiple_of(i * pair, pair), pair)
            to = pl.ds(pl.multiple_of(base + i * pair, 16), pair)
            g = source[at, :].astype(F32) * factor
            low = jnp.where(keep_low, pltpu.roll(g, pair - KERNEL_DILATION, 0), 0.0)
            high = jnp.where(keep_high, pltpu.roll(g, KERNEL_DILATION, 0), 0.0)
            for kx, value in enumerate((low, g, high)):
                t = 3 * ky + kx
                sh[to, t * out_channels : (t + 1) * out_channels] = value.astype(BF16)
            return 0

        lax.fori_loop(start, stop, rows, 0)

    pairs = pixels // pair

    own_flag = alive[0:1, 0:1]

    def inside(delta):
        there = space + delta
        return jnp.where((there >= 0) & (there < space_n), 1.0, 0.0)

    def build_halo(source, base, ky, flag):
        low, high = (1, 2) if ky == 0 else (-2, -1)
        build(source, base, ky, flag * inside(low), 0, pairs // 2)
        build(source, base, ky, flag * inside(high), pairs // 2, pairs)

    def term(ki):
        ky = KY_ORDER[ki]

        def one(v, _):
            r = lax.dot_general(
                fb[v], sh[:, ky * width : (ky + 1) * width], (((0,), (0,)), ((), ())), preferred_element_type=F32
            )
            for kx in range(3):
                for h in range(2):
                    start = kx * out_channels + h * 128
                    acc[ki, kx, h, v] = r[:, start : start + 128].reshape(SIDE, SIDE, block // (SIDE * SIDE), 128)
            return 0

        lax.fori_loop(0, SIDE, one, 0)

    stages = (rb1, rb2, rb3)

    def view(wave, kx, h, stage, value):
        lo, n = WAVES[wave]
        order = AXIS_ORDERS[kx]
        index = {a: slice(None) for a in "xyz"}
        for done in order[:stage]:
            index[done] = me[done]
        index[order[stage]] = value
        return (pl.ds(lo, n), kx, h, index["x"], index["z"], index["y"])

    rings = {}

    def ring(wave, kx, stage):
        if (wave, kx, stage) not in rings:
            rings[wave, kx, stage] = make_ring(wave, kx, stage)
        return rings[wave, kx, stage]

    def make_ring(wave, kx, stage):
        lo, n = WAVES[wave]
        axis = AXIS_ORDERS[kx][stage]
        at = me[axis]
        nxt, two, prv = (lax.rem(at + d, SIDE) for d in (1, 2, 3))
        sends = [(0, two, 1), (1, nxt, 1), (0, nxt, 1), (1, two, -1), (0, prv, -1), (1, prv, -1)]
        copies = []
        for m, (h, value, way) in enumerate(sends):
            copies.append(
                remote(
                    acc.at[view(wave, kx, h, stage, value)],
                    stages[stage].at[pl.ds(lo, n), kx, m],
                    st_s.at[wave, kx, stage, m],
                    st_r.at[wave, kx, stage, m],
                    step(axis, way),
                )
            )
        return copies

    def begin(wave, stage):
        for kx in range(3):
            c = ring(wave, kx, stage)
            for m in (0, 3, 1, 4):
                c[m].start()

    def middle(wave, stage):
        lo, n = WAVES[wave]
        buf = stages[stage]
        for kx in range(3):
            axis = AXIS_ORDERS[kx][stage]
            c = ring(wave, kx, stage)
            for arrived, onward, h, delta in ((0, 2, 0, 1), (3, 5, 1, 3)):
                c[arrived].wait_recv()
                at = view(wave, kx, h, stage, lax.rem(me[axis] + delta, SIDE))
                acc[at] = acc[at] + buf[pl.ds(lo, n), kx, arrived]
                c[onward].start()

    def finish(wave, stage):
        lo, n = WAVES[wave]
        buf = stages[stage]
        for kx in range(3):
            axis = AXIS_ORDERS[kx][stage]
            c = ring(wave, kx, stage)
            for h, parts in ((0, (4, 2)), (1, (1, 5))):
                for m in parts:
                    c[m].wait_recv()
                at = view(wave, kx, h, stage, me[axis])
                got = [buf[pl.ds(lo, n), kx, m] for m in parts]
                total = acc[at] + got[0] + got[1]
                if stage < 2:
                    acc[at] = total
                else:
                    total = total * inverse
                    for i in range(n):
                        t = 3 * KY_ORDER[lo + i] + kx
                        wgs[h, pl.ds(t, 16, 9), :] = total[i]

    def drain():
        for wave in range(len(WAVES)):
            for stage in range(3):
                for kx in range(3):
                    for c in ring(wave, kx, stage):
                        c.wait_send()

    chans = wf32.shape[1] // 9

    def relayout(i0, i1):
        def one(i, _):
            at = pl.ds(pl.multiple_of(i * chans * 9, 16), chans * 9)
            for h in range(out_channels // 128):
                wf32[h] = wraw[at, h * 128 : (h + 1) * 128].astype(F32)
            to = pl.ds(pl.multiple_of(i * chans, 16), chans)
            for t in range(9):
                for h in range(out_channels // 128):
                    piece = wf32[h, pl.ds(t, chans, 9), :]
                    lane = t * out_channels + h * 128
                    wt[to, lane : lane + 128] = piece.astype(BF16)
            return 0

        lax.fori_loop(i0, i1, one, 0)

    gblock = gbuf.shape[2]
    gcount = gf.shape[1] // gblock

    def gf_copy(b):
        return pltpu.make_async_copy(
            gbuf.at[b % 2], gf.at[:, pl.ds(pl.multiple_of(b * gblock, gblock), gblock)], gf_sem.at[b % 2]
        )

    def back(b0, b1):
        for b in range(b0, b1):
            if b >= 2:
                gf_copy(b - 2).wait()
            r = lax.dot_general(
                sh[0:pixels, :], wt[pl.ds(b * gblock, gblock), :], (((1,), (1,)), ((), ())), preferred_element_type=F32
            )
            gbuf[b % 2] = (r * inverse[0:1, 0:1]).astype(BF16)
            gf_copy(b).start()

    blocks = wt.shape[0] // chans
    own_grad.wait()
    build(own_g.at[0], 0, 1, own_flag, 0, pairs)
    for c in flag_copies:
        c.wait_recv()
    total = alive[...]
    for d in range(1, dp_n):
        total = total + flags[d - 1]
    inverse = (1.0 / total)[0:1, :]
    par_flag = flags[6 * (1 - k)][0:1, 0:1]
    centre.wait_recv()
    build(par_g.at[0], pixels, 1, par_flag, 0, pairs)
    for i, c in enumerate(features):
        if i % 2:
            c.wait()
        else:
            c.wait_recv()
    term(0)
    begin(0, 0)
    forwards = []
    for i, c in enumerate(halos):
        c.wait_recv()
        where = (1 + i // 2, first if i % 2 == 0 else last)
        f = remote(own_g.at[where], par_g.at[where], fwd_s.at[i], fwd_r.at[i], partner)
        f.start()
        forwards.append(f)
    build_halo(own_g.at[1], 0, 0, own_flag)
    build_halo(own_g.at[2], 0, 2, own_flag)
    for f in forwards:
        f.wait_recv()
    build_halo(par_g.at[1], pixels, 0, par_flag)
    build_halo(par_g.at[2], pixels, 2, par_flag)
    middle(0, 0)
    term(1)
    term(2)
    begin(1, 0)
    finish(0, 0)
    begin(0, 1)
    weights.wait()
    relayout(0, blocks // 2)
    middle(0, 1)
    relayout(blocks // 2, blocks)
    middle(1, 0)
    finish(0, 1)
    begin(0, 2)
    back(0, 2)
    middle(0, 2)
    back(2, 4)
    finish(1, 0)
    begin(1, 1)
    finish(0, 2)
    back(4, 6)
    middle(1, 1)
    back(6, 7)
    finish(1, 1)
    begin(1, 2)
    back(7, gcount)
    middle(1, 2)
    finish(1, 2)
    for h in range(out_channels // 128):
        wg[:, h * 128 : (h + 1) * 128] = wgs[h]
    gf_copy(gcount - 2).wait()
    gf_copy(gcount - 1).wait()
    for c in halos + [centre] + flag_copies + forwards:
        c.wait_send()
    for c in features[::2]:
        c.wait_send()
    drain()


def fused(features, grad_out, weight, alive):
    members, rows, cols, in_channels = features.shape
    out_channels = grad_out.shape[-1]
    pixels = rows * cols
    block = in_channels // (2 * SIDE)
    sub = block // 16
    chans = 128
    gblock = 256
    dma = pltpu.SemaphoreType.DMA
    anyspace = pl.BlockSpec(memory_space=pl.ANY)
    vmem = pl.BlockSpec(memory_space=pltpu.VMEM)
    scratch = [
        pltpu.VMEM((3, pixels, out_channels), BF16),
        pltpu.VMEM((3, pixels, out_channels), BF16),
        pltpu.VMEM((SIDE, 2 * pixels, block), BF16),
        pltpu.VMEM((2 * pixels, 9 * out_channels), BF16),
        pltpu.VMEM(weight.shape, BF16),
        pltpu.VMEM((out_channels // 128, 9 * chans, 128), F32),
        pltpu.VMEM((out_channels // 128, sub * 9, 128), F32),
        pltpu.VMEM((in_channels, 9 * out_channels), BF16),
        pltpu.VMEM((3, 3, 2, SIDE, SIDE, SIDE, sub, 128), F32),
        pltpu.VMEM((3, 3, 6, SIDE, SIDE, sub, 128), F32),
        pltpu.VMEM((3, 3, 6, SIDE, sub, 128), F32),
        pltpu.VMEM((3, 3, 6, sub, 128), F32),
        pltpu.VMEM((2 * SIDE - 1, 8, 128), F32),
        pltpu.VMEM((2, pixels, gblock), BF16),
        dma((4,)), dma((4,)), dma((4,)), dma((4,)), dma(()), dma(()), dma((SIDE,)), dma((SIDE,)),
        dma((2 * SIDE - 1,)), dma((2 * SIDE - 1,)),
        dma((len(WAVES), 3, 3, 6)), dma((len(WAVES), 3, 3, 6)), dma((2 + SIDE,)), dma((2,)),
    ]
    flag = jnp.broadcast_to(alive.astype(F32).reshape(1, 1), (8, 128))
    weight_grad, grad_features = pl.pallas_call(
        functools.partial(body, cols),
        out_shape=(
            jax.ShapeDtypeStruct((sub * 9, out_channels), F32),
            jax.ShapeDtypeStruct((pixels, in_channels), BF16),
        ),
        in_specs=[anyspace, anyspace, anyspace, vmem],
        out_specs=(vmem, anyspace),
        scratch_shapes=scratch,
        compiler_params=pltpu.CompilerParams(
            collective_id=0, has_side_effects=True, vmem_limit_bytes=66_000_000
        ),
    )(features.reshape(pixels, in_channels), grad_out.reshape(pixels, out_channels), weight, flag)
    return weight_grad, grad_features.reshape(features.shape)


def solution(mesh):
    in_specs = (P("dp", "space", None, None), P("dp", "space", None, None), P(), P("dp"))
    out_specs = (P(("dp", "space"), None), P("dp", "space", None, None))
    return jax.shard_map(fused, mesh=mesh, in_specs=in_specs, out_specs=out_specs, check_vma=False)
```

```python
import functools

import jax
import jax.numpy as jnp
from jax import lax
from jax.experimental import pallas as pl
from jax.experimental.pallas import tpu as pltpu
from jax.sharding import PartitionSpec as P

KERNEL_DILATION = 18
MESH = pl.DeviceIdType.MESH
F32 = jnp.float32
BF16 = jnp.bfloat16

SIDE = 4
KY_ORDER = (1, 0, 2)
WAVES = ((0, 1), (1, 1), (2, 1))
AXIS_ORDERS = ("xyz", "yzx", "zxy")


def body(
    cols,
    feat, grad, weight, alive,
    wg, gf,
    own_g, par_g, fb, sh, wraw, wf32, wgs, wt, acc, rb1, rb2, rb3, flags, gbuf,
    halo_s, halo_r, fwd_s, fwd_r, cen_s, cen_r, fea_s, fea_r, flag_s, flag_r, st_s, st_r, loc, gf_sem,
):
    pixels = grad.shape[0]
    half = pixels // 2
    out_channels = grad.shape[1]
    width = 3 * out_channels
    block = fb.shape[2]
    dp, space = lax.axis_index("dp"), lax.axis_index("space")
    dp_n, space_n = 2 * SIDE, SIDE * SIDE
    x, k = dp // 2, dp % 2
    z, y = space // SIDE, space % SIDE
    me = {"x": x, "y": y, "z": z}

    def dev(d, s):
        return {"dp": d, "space": s}

    def step(axis, delta):
        moved = dict(me)
        moved[axis] = lax.rem(me[axis] + (delta + SIDE), SIDE)
        return dev(2 * moved["x"] + k, SIDE * moved["z"] + moved["y"])

    def along_space(delta):
        return dev(dp, lax.rem(space + (delta + space_n), space_n))

    def along_dp(delta):
        return dev(lax.rem(dp + delta, dp_n), space)

    partner = dev(2 * x + (1 - k), space)

    barrier = pltpu.get_barrier_semaphore()
    peers = [along_dp(d) for d in range(1, dp_n)]
    peers += [along_space(d) for d in (1, -1, 2, -2)]
    peers += [step(a, d) for a in "yz" for d in (1, -1)]
    for p in peers:
        pl.semaphore_signal(barrier, inc=1, device_id=p, device_id_type=MESH)

    def feature_block(v, kk):
        return feat.at[:, pl.ds(pl.multiple_of((2 * v + kk) * block, block), block)]

    own_grad = pltpu.make_async_copy(grad, own_g.at[0], loc.at[0])
    own_grad.start()
    own_features = [
        pltpu.make_async_copy(feature_block(v, k), fb.at[v, pl.ds(0, pixels)], loc.at[2 + v]) for v in range(SIDE)
    ]
    for c in own_features:
        c.start()
    weights = pltpu.make_async_copy(weight, wraw, loc.at[1])
    weights.start()

    pair = 2 * cols
    position = lax.broadcasted_iota(jnp.int32, (pair, out_channels), 0)
    column = jnp.where(position >= cols, position - cols, position)
    keep_low = column < cols - KERNEL_DILATION
    keep_high = column >= KERNEL_DILATION

    def build(source, base, ky, factor, start, stop):
        def rows(i, _):
            at = pl.ds(pl.multiple_of(i * pair, pair), pair)
            to = pl.ds(pl.multiple_of(base + i * pair, 16), pair)
            g = source[at, :].astype(F32) * factor
            low = jnp.where(keep_low, pltpu.roll(g, pair - KERNEL_DILATION, 0), 0.0)
            high = jnp.where(keep_high, pltpu.roll(g, KERNEL_DILATION, 0), 0.0)
            for kx, value in enumerate((low, g, high)):
                t = 3 * ky + kx
                sh[to, t * out_channels : (t + 1) * out_channels] = value.astype(BF16)
            return 0

        lax.fori_loop(start, stop, rows, 0)

    pairs = pixels // pair

    own_flag = alive[0:1, 0:1]

    def inside(delta):
        there = space + delta
        return jnp.where((there >= 0) & (there < space_n), 1.0, 0.0)

    def build_halo(source, base, ky, flag):
        low, high = (1, 2) if ky == 0 else (-2, -1)
        build(source, base, ky, flag * inside(low), 0, pairs // 2)
        build(source, base, ky, flag * inside(high), pairs // 2, pairs)

    own_grad.wait()
    build(own_g.at[0], 0, 1, own_flag, 0, pairs)
    pl.semaphore_wait(barrier, len(peers))

    def remote(src, dst, s_sem, r_sem, to):
        return pltpu.make_async_remote_copy(
            src_ref=src, dst_ref=dst, send_sem=s_sem, recv_sem=r_sem, device_id=to, device_id_type=MESH
        )

    first, last = pl.ds(0, half), pl.ds(half, half)
    halos = [
        remote(grad.at[last], own_g.at[1, first], halo_s.at[0], halo_r.at[0], along_space(-1)),
        remote(grad.at[first], own_g.at[1, last], halo_s.at[1], halo_r.at[1], along_space(-2)),
        remote(grad.at[last], own_g.at[2, first], halo_s.at[2], halo_r.at[2], along_space(2)),
        remote(grad.at[first], own_g.at[2, last], halo_s.at[3], halo_r.at[3], along_space(1)),
    ]
    for c in halos:
        c.start()
    centre = remote(grad, par_g.at[0], cen_s, cen_r, partner)
    centre.start()
    flag_copies = [
        remote(alive, flags.at[d - 1], flag_s.at[d - 1], flag_r.at[d - 1], along_dp(d)) for d in range(1, dp_n)
    ]
    for c in flag_copies:
        c.start()

    features = [
        remote(feature_block(v, 1 - k), fb.at[v, pl.ds(pixels, pixels)], fea_s.at[v], fea_r.at[v], partner)
        for v in range(SIDE)
    ]
    for c in features:
        c.start()

    def term(ki):
        ky = KY_ORDER[ki]

        def one(v, _):
            r = lax.dot_general(
                fb[v], sh[:, ky * width : (ky + 1) * width], (((0,), (0,)), ((), ())), preferred_element_type=F32
            )
            for kx in range(3):
                for h in range(2):
                    start = kx * out_channels + h * 128
                    acc[ki, kx, h, v] = r[:, start : start + 128].reshape(SIDE, SIDE, block // (SIDE * SIDE), 128)
            return 0

        lax.fori_loop(0, SIDE, one, 0)

    stages = (rb1, rb2, rb3)

    def view(wave, kx, h, stage, value):
        lo, n = WAVES[wave]
        order = AXIS_ORDERS[kx]
        index = {a: slice(None) for a in "xyz"}
        for done in order[:stage]:
            index[done] = me[done]
        index[order[stage]] = value
        return (pl.ds(lo, n), kx, h, index["x"], index["z"], index["y"])

    rings = {}

    def ring(wave, kx, stage):
        if (wave, kx, stage) not in rings:
            rings[wave, kx, stage] = make_ring(wave, kx, stage)
        return rings[wave, kx, stage]

    def make_ring(wave, kx, stage):
        lo, n = WAVES[wave]
        axis = AXIS_ORDERS[kx][stage]
        at = me[axis]
        nxt, two, prv = (lax.rem(at + d, SIDE) for d in (1, 2, 3))
        sends = [(0, two, 1), (1, nxt, 1), (0, nxt, 1), (1, two, -1), (0, prv, -1), (1, prv, -1)]
        copies = []
        for m, (h, value, way) in enumerate(sends):
            copies.append(
                remote(
                    acc.at[view(wave, kx, h, stage, value)],
                    stages[stage].at[pl.ds(lo, n), kx, m],
                    st_s.at[wave, kx, stage, m],
                    st_r.at[wave, kx, stage, m],
                    step(axis, way),
                )
            )
        return copies

    def begin(wave, stage, kxs=(0, 1, 2)):
        for kx in kxs:
            c = ring(wave, kx, stage)
            for m in (0, 3, 1, 4):
                c[m].start()

    def middle(wave, stage, kxs=(0, 1, 2)):
        lo, n = WAVES[wave]
        buf = stages[stage]
        for kx in kxs:
            axis = AXIS_ORDERS[kx][stage]
            c = ring(wave, kx, stage)
            for arrived, onward, h, delta in ((0, 2, 0, 1), (3, 5, 1, 3)):
                c[arrived].wait_recv()
                at = view(wave, kx, h, stage, lax.rem(me[axis] + delta, SIDE))
                acc[at] = acc[at] + buf[pl.ds(lo, n), kx, arrived]
                c[onward].start()

    def finish(wave, stage):
        lo, n = WAVES[wave]
        buf = stages[stage]
        for kx in range(3):
            axis = AXIS_ORDERS[kx][stage]
            c = ring(wave, kx, stage)
            for h, parts in ((0, (4, 2)), (1, (1, 5))):
                for m in parts:
                    c[m].wait_recv()
                at = view(wave, kx, h, stage, me[axis])
                got = [buf[pl.ds(lo, n), kx, m] for m in parts]
                total = acc[at] + got[0] + got[1]
                if stage < 2:
                    acc[at] = total
                else:
                    total = total * inverse
                    for i in range(n):
                        t = 3 * KY_ORDER[lo + i] + kx
                        wgs[h, pl.ds(t, 16, 9), :] = total[i]

    def drain():
        for wave in range(len(WAVES)):
            for stage in range(3):
                for kx in range(3):
                    for c in ring(wave, kx, stage):
                        c.wait_send()

    chans = wf32.shape[1] // 9

    def relayout(i0, i1):
        def one(i, _):
            at = pl.ds(pl.multiple_of(i * chans * 9, 16), chans * 9)
            for h in range(out_channels // 128):
                wf32[h] = wraw[at, h * 128 : (h + 1) * 128].astype(F32)
            to = pl.ds(pl.multiple_of(i * chans, 16), chans)
            for t in range(9):
                for h in range(out_channels // 128):
                    piece = wf32[h, pl.ds(t, chans, 9), :]
                    lane = t * out_channels + h * 128
                    wt[to, lane : lane + 128] = piece.astype(BF16)
            return 0

        lax.fori_loop(i0, i1, one, 0)

    gblock = gbuf.shape[2]
    gcount = gf.shape[1] // gblock

    def gf_copy(b):
        return pltpu.make_async_copy(
            gbuf.at[b % 2], gf.at[:, pl.ds(pl.multiple_of(b * gblock, gblock), gblock)], gf_sem.at[b % 2]
        )

    def back(b0, b1):
        for b in range(b0, b1):
            if b >= 2:
                gf_copy(b - 2).wait()
            r = lax.dot_general(
                sh[0:pixels, :], wt[pl.ds(b * gblock, gblock), :], (((1,), (1,)), ((), ())), preferred_element_type=F32
            )
            gbuf[b % 2] = (r * inverse[0:1, 0:1]).astype(BF16)
            gf_copy(b).start()

    blocks = wt.shape[0] // chans
    for c in flag_copies:
        c.wait_recv()
    total = alive[...]
    for d in range(1, dp_n):
        total = total + flags[d - 1]
    inverse = (1.0 / total)[0:1, :]
    par_flag = flags[6 * (1 - k)][0:1, 0:1]
    centre.wait_recv()
    build(par_g.at[0], pixels, 1, par_flag, 0, pairs)
    for c in own_features:
        c.wait()
    for c in features:
        c.wait_recv()
    term(0)
    begin(0, 0, (0, 2))
    weights.wait()
    relayout(0, 5)
    forwards = []
    for i, c in enumerate(halos):
        c.wait_recv()
        where = (1 + i // 2, first if i % 2 == 0 else last)
        f = remote(own_g.at[where], par_g.at[where], fwd_s.at[i], fwd_r.at[i], partner)
        f.start()
        forwards.append(f)
    begin(0, 0, (1,))
    build_halo(own_g.at[1], 0, 0, own_flag)
    build_halo(own_g.at[2], 0, 2, own_flag)
    middle(0, 0, (0, 2))
    for f in forwards[:2]:
        f.wait_recv()
    build_halo(par_g.at[1], pixels, 0, par_flag)
    term(1)
    begin(1, 0)
    for f in forwards[2:]:
        f.wait_recv()
    build_halo(par_g.at[2], pixels, 2, par_flag)
    term(2)
    begin(2, 0)
    middle(0, 0, (1,))
    relayout(5, 8)
    middle(1, 0)
    finish(0, 0)
    begin(0, 1)
    relayout(8, 12)
    middle(0, 1)
    relayout(12, 14)
    middle(2, 0)
    finish(1, 0)
    begin(1, 1)
    relayout(14, blocks)
    finish(0, 1)
    begin(0, 2)
    back(0, 1)
    middle(1, 1)
    finish(2, 0)
    begin(2, 1)
    middle(0, 2)
    back(1, 3)
    finish(1, 1)
    begin(1, 2)
    middle(2, 1)
    finish(0, 2)
    back(3, 5)
    finish(2, 1)
    begin(2, 2)
    middle(1, 2)
    back(5, 6)
    middle(2, 2)
    finish(1, 2)
    back(6, gcount)
    finish(2, 2)
    for h in range(out_channels // 128):
        wg[:, h * 128 : (h + 1) * 128] = wgs[h]
    gf_copy(gcount - 2).wait()
    gf_copy(gcount - 1).wait()
    for c in halos + [centre] + flag_copies + forwards:
        c.wait_send()
    for c in features:
        c.wait_send()
    drain()


def fused(features, grad_out, weight, alive):
    members, rows, cols, in_channels = features.shape
    out_channels = grad_out.shape[-1]
    pixels = rows * cols
    block = in_channels // (2 * SIDE)
    sub = block // 16
    chans = 128
    gblock = 256
    dma = pltpu.SemaphoreType.DMA
    anyspace = pl.BlockSpec(memory_space=pl.ANY)
    vmem = pl.BlockSpec(memory_space=pltpu.VMEM)
    scratch = [
        pltpu.VMEM((3, pixels, out_channels), BF16),
        pltpu.VMEM((3, pixels, out_channels), BF16),
        pltpu.VMEM((SIDE, 2 * pixels, block), BF16),
        pltpu.VMEM((2 * pixels, 9 * out_channels), BF16),
        pltpu.VMEM(weight.shape, BF16),
        pltpu.VMEM((out_channels // 128, 9 * chans, 128), F32),
        pltpu.VMEM((out_channels // 128, sub * 9, 128), F32),
        pltpu.VMEM((in_channels, 9 * out_channels), BF16),
        pltpu.VMEM((3, 3, 2, SIDE, SIDE, SIDE, sub, 128), F32),
        pltpu.VMEM((3, 3, 6, SIDE, SIDE, sub, 128), F32),
        pltpu.VMEM((3, 3, 6, SIDE, sub, 128), F32),
        pltpu.VMEM((3, 3, 6, sub, 128), F32),
        pltpu.VMEM((2 * SIDE - 1, 8, 128), F32),
        pltpu.VMEM((2, pixels, gblock), BF16),
        dma((4,)), dma((4,)), dma((4,)), dma((4,)), dma(()), dma(()), dma((SIDE,)), dma((SIDE,)),
        dma((2 * SIDE - 1,)), dma((2 * SIDE - 1,)),
        dma((len(WAVES), 3, 3, 6)), dma((len(WAVES), 3, 3, 6)), dma((2 + SIDE,)), dma((2,)),
    ]
    flag = jnp.broadcast_to(alive.astype(F32).reshape(1, 1), (8, 128))
    weight_grad, grad_features = pl.pallas_call(
        functools.partial(body, cols),
        out_shape=(
            jax.ShapeDtypeStruct((sub * 9, out_channels), F32),
            jax.ShapeDtypeStruct((pixels, in_channels), BF16),
        ),
        in_specs=[anyspace, anyspace, anyspace, vmem],
        out_specs=(vmem, anyspace),
        scratch_shapes=scratch,
        compiler_params=pltpu.CompilerParams(
            collective_id=0, has_side_effects=True, vmem_limit_bytes=66_000_000
        ),
    )(features.reshape(pixels, in_channels), grad_out.reshape(pixels, out_channels), weight, flag)
    return weight_grad, grad_features.reshape(features.shape)


def solution(mesh):
    in_specs = (P("dp", "space", None, None), P("dp", "space", None, None), P(), P("dp"))
    out_specs = (P(("dp", "space"), None), P("dp", "space", None, None))
    return jax.shard_map(fused, mesh=mesh, in_specs=in_specs, out_specs=out_specs, check_vma=False)
```
